768 devices in a mesh: fsdp: 192 (over x, z_lo, y, core), tp: 4 (over z_hi).
Axes of the slice: x: 4, y: 8, z: 12 (z_hi: 4, z_lo: 3; z = z_hi * 3 + z_lo), core: 2. Of those that a mesh axis runs over, the one named last changes fastest.
Arguments:
- tokens: bfloat16 [384, 8192], P('fsdp', 'tp'), may hold values from -6 to 6
- gate_weight: bfloat16 [27648, 8192], P('fsdp', 'tp'), may hold values from -0.0625 to 0.0625
- up_weight: bfloat16 [27648, 8192], P('fsdp', 'tp'), may hold values from -0.0625 to 0.0625
- down_weight: bfloat16 [27648, 8192], P('fsdp', 'tp'), may hold values from -0.0390625 to 0.0390625
Outputs:
- mixed: bfloat16 [384, 8192], P('fsdp', 'tp')
The draws below stay inside these ranges and needn't reach their ends.
All inputs are finite; a program needn't handle non-finite values.
Results may differ from the reference program's by a relative error of at most 0.0049.
Values may be sent and summed in bfloat16 or wider, within the bound.
No kernel may reach another device: no remote copies, remote signals or barrier semaphores. Data moves between devices by JAX's collectives and lax.ppermute only.
A program may use at most 32 MiB of HBM per device.

```python
import jax
import jax.numpy as jnp

D = 8192
FF = 27648
TOKENS = 384


def block_levels(key, shape, shards, least, high):
    gain, own = 1.0, jax.random.fold_in(key, 6)
    for axis_at, shards_of in shards:
        steps = jnp.exp(jax.random.uniform(jax.random.fold_in(own, axis_at), (shards_of,), jnp.float32, least / len(shards), high / len(shards)))
        gain = gain * jnp.repeat(steps, shape[axis_at] // shards_of).reshape([-1 if axis == axis_at else 1 for axis in range(len(shape))])
    return gain


def centred(stream_key, extent, deviation, limit, pieces=(), held_as=jnp.bfloat16):
    entries = jax.random.normal(stream_key, extent, jnp.float32) * deviation
    if len(pieces) > 0:
        entries = block_levels(stream_key, extent, pieces, -0.22, 0.18) * entries
    return jnp.clip(entries, min=-limit, max=limit).astype(held_as)


def setup_inputs(seed: int = 0) -> dict:
    streams_of = jax.random.split(jax.random.key(seed), 5)
    tokens = centred(streams_of[0], (TOKENS, D), 1.0, 6.0, ((0, 192), (1, 4)))
    gate_weight = centred(streams_of[1], (FF, D), D ** -0.5, 0.0625, ((0, 192), (1, 4)))
    up_weight = centred(streams_of[2], (FF, D), D ** -0.5, 0.0625, ((0, 192), (1, 4)))
    down_weight = centred(streams_of[3], (FF, D), FF ** -0.5, 0.0390625, ((0, 192), (1, 4)))
    return {"tokens": tokens, "gate_weight": gate_weight, "up_weight": up_weight, "down_weight": down_weight}


def reference(tokens, gate_weight, up_weight, down_weight):
    gate = jnp.dot(tokens, gate_weight.T, preferred_element_type=jnp.float32)
    up = jnp.dot(tokens, up_weight.T, preferred_element_type=jnp.float32)
    hidden = (jax.nn.silu(gate) * up).astype(jnp.bfloat16)
    mixed = jnp.dot(hidden, down_weight, preferred_element_type=jnp.float32)
    return mixed.astype(jnp.bfloat16)
```

```python
import jax
import jax.numpy as jnp
from jax import lax
from jax.sharding import Mesh
from jax.sharding import PartitionSpec as P

CHIPS = "chips"
CORE = "core"
TP = "tp"


def body(tokens, gate_weight, up_weight, down_weight):
    chips = lax.axis_size(CHIPS)
    tp = lax.axis_size(TP)
    mine, width = tokens.shape
    hidden_width = gate_weight.shape[0]
    swap = [(0, 1), (1, 0)]
    rows = chips * mine

    spread = jnp.broadcast_to(tokens[None], (chips, mine, width))
    own = lax.all_to_all(spread, CHIPS, split_axis=0, concat_axis=0, tiled=True)
    own = own.reshape(rows, width)
    other = lax.ppermute(own, CORE, swap)
    block_rows = jnp.concatenate([own, other], axis=0)

    contract = (((1,), (1,)), ((), ()))
    gate_part = lax.dot_general(
        gate_weight, block_rows, contract, preferred_element_type=jnp.float32
    )
    up_part = lax.dot_general(up_weight, block_rows, contract, preferred_element_type=jnp.float32)
    share = hidden_width // tp
    parts = jnp.concatenate(
        [gate_part.reshape(tp, share, 2 * rows), up_part.reshape(tp, share, 2 * rows)], axis=1
    )
    parts = lax.all_to_all(
        parts.astype(jnp.bfloat16), TP, split_axis=0, concat_axis=0, tiled=True
    )
    sums = jnp.sum(parts.astype(jnp.float32), axis=0)
    quarter = (jax.nn.silu(sums[:share]) * sums[share:]).astype(jnp.bfloat16)
    hidden = lax.all_gather(quarter, TP, axis=0, tiled=True)

    down_terms = lax.dot_general(
        hidden, down_weight, (((0,), (0,)), ((), ())), preferred_element_type=jnp.float32
    )
    sent = lax.ppermute(down_terms[rows:].astype(jnp.bfloat16), CORE, swap)
    chip_terms = (down_terms[:rows] + sent.astype(jnp.float32)).astype(jnp.bfloat16)
    chip_terms = lax.all_to_all(
        chip_terms.reshape(chips, mine, width), CHIPS, split_axis=0, concat_axis=0, tiled=True
    )
    return jnp.sum(chip_terms.astype(jnp.float32), axis=0).astype(jnp.bfloat16)


def solution(mesh):
    cores = 2
    fsdp, tp = mesh.devices.shape
    fine = Mesh(mesh.devices.reshape(fsdp // cores, cores, tp), (CHIPS, CORE, TP))
    placed = P((CHIPS, CORE), TP)
    return jax.shard_map(
        body, mesh=fine, in_specs=(placed,) * 4, out_specs=placed, check_vma=False
    )
```

```python
import jax
import jax.numpy as jnp
from jax import lax
from jax.sharding import Mesh
from jax.sharding import PartitionSpec as P

CHIPS = "chips"
CORE = "core"
TP = "tp"


def body(tokens, gate_weight, up_weight, down_weight):
    chips = lax.axis_size(CHIPS)
    tp = lax.axis_size(TP)
    mine, width = tokens.shape
    hidden_width = 2 * gate_weight.shape[0]
    share = hidden_width // tp
    swap = [(0, 1), (1, 0)]
    rows = chips * mine

    gate_weight, up_weight, down_weight = (
        jnp.concatenate([part, lax.ppermute(part, CORE, swap)], axis=0)
        for part in (gate_weight, up_weight, down_weight)
    )
    spread = jnp.broadcast_to(tokens[None], (chips, mine, width))
    block_rows = lax.all_to_all(spread, CHIPS, split_axis=0, concat_axis=0, tiled=True)
    block_rows = block_rows.reshape(rows, width)

    contract = (((1,), (1,)), ((), ()))
    gate_part = lax.dot_general(
        gate_weight, block_rows, contract, preferred_element_type=jnp.float32
    )
    up_part = lax.dot_general(up_weight, block_rows, contract, preferred_element_type=jnp.float32)
    parts = jnp.concatenate([gate_part, up_part], axis=1).reshape(tp, share, 2 * rows)
    parts = lax.all_to_all(
        parts.astype(jnp.bfloat16), TP, split_axis=0, concat_axis=0, tiled=True
    )
    sums = jnp.sum(parts.astype(jnp.float32), axis=0)
    quarter = (jax.nn.silu(sums[:, :rows]) * sums[:, rows:]).astype(jnp.bfloat16)
    hidden = lax.all_gather(quarter, TP, axis=0, tiled=True)

    chip_terms = lax.dot_general(
        hidden, down_weight, (((0,), (0,)), ((), ())), preferred_element_type=jnp.float32
    ).astype(jnp.bfloat16)
    chip_terms = lax.all_to_all(
        chip_terms.reshape(chips, mine, width), CHIPS, split_axis=0, concat_axis=0, tiled=True
    )
    return jnp.sum(chip_terms.astype(jnp.float32), axis=0).astype(jnp.bfloat16)


def solution(mesh):
    cores = 2
    fsdp, tp = mesh.devices.shape
    fine = Mesh(mesh.devices.reshape(fsdp // cores, cores, tp), (CHIPS, CORE, TP))
    placed = P((CHIPS, CORE), TP)
    return jax.shard_map(
        body, mesh=fine, in_specs=(placed,) * 4, out_specs=placed, check_vma=False
    )
```

```python
import jax
import jax.numpy as jnp
from jax import lax
from jax.sharding import Mesh
from jax.sharding import PartitionSpec as P

X = "x"
PLANE = "plane"
CORE = "core"
TP = "tp"


def exchange(chunks, axes):
    return lax.all_to_all(chunks, axes, split_axis=0, concat_axis=0, tiled=True)


def body(tokens, gate_weight, up_weight, down_weight):
    line, plane, tp = lax.axis_size(X), lax.axis_size(PLANE), lax.axis_size(TP)
    mine, width = tokens.shape
    hidden_width = 2 * gate_weight.shape[0]
    share = hidden_width // tp
    column = plane * mine
    rows = line * column
    swap = [(0, 1), (1, 0)]

    gate_weight, up_weight, down_weight = (
        jnp.concatenate([part, lax.ppermute(part, CORE, swap)], axis=0)
        for part in (gate_weight, up_weight, down_weight)
    )
    block = exchange(jnp.broadcast_to(tokens[None], (plane, mine, width)), PLANE)
    block = block.reshape(column, width)
    block = exchange(jnp.broadcast_to(block[None], (line, column, width)), X)
    block = block.reshape(rows, width)

    contract = (((1,), (1,)), ((), ()))
    gate_part = lax.dot_general(gate_weight, block, contract, preferred_element_type=jnp.float32)
    up_part = lax.dot_general(up_weight, block, contract, preferred_element_type=jnp.float32)
    parts = jnp.concatenate([gate_part, up_part], axis=1).reshape(tp, share, 2 * rows)
    parts = parts.astype(jnp.bfloat16)

    parts, down_weight = lax.optimization_barrier((parts, down_weight))
    down_weights = [down_weight] + [
        lax.ppermute(down_weight, X, [((i + step) % line, i) for i in range(line)])
        for step in range(1, line)
    ]
    parts = exchange(parts, TP)
    sums = jnp.sum(parts.astype(jnp.float32), axis=0)
    quarter = (jax.nn.silu(sums[:, :rows]) * sums[:, rows:]).astype(jnp.bfloat16)
    quarter = quarter.reshape(share, line, column).transpose(1, 0, 2)
    spread = jnp.broadcast_to(quarter[:, None], (line, tp, share, column))
    hidden = exchange(spread.reshape(line * tp, share, column), (X, TP))
    hidden = hidden.reshape(line, hidden_width, column)

    here = lax.axis_index(X)
    hidden = jnp.concatenate(
        [
            lax.dynamic_index_in_dim(hidden, lax.rem(here + step, line), 0, keepdims=False)
            for step in range(line)
        ],
        axis=0,
    )
    terms = lax.dot_general(
        hidden,
        jnp.concatenate(down_weights, axis=0),
        (((0,), (0,)), ((), ())),
        preferred_element_type=jnp.float32,
    ).astype(jnp.bfloat16)
    terms = exchange(terms.reshape(plane, mine, width), PLANE)
    return jnp.sum(terms.astype(jnp.float32), axis=0).astype(jnp.bfloat16)


def solution(mesh):
    line, cores = 4, 2
    fsdp, tp = mesh.devices.shape
    fine = Mesh(
        mesh.devices.reshape(line, fsdp // (line * cores), cores, tp), (X, PLANE, CORE, TP)
    )
    placed = P((X, PLANE, CORE), TP)
    return jax.shard_map(
        body, mesh=fine, in_specs=(placed,) * 4, out_specs=placed, check_vma=False
    )
```

```python
import functools

import jax
import jax.numpy as jnp
from jax import lax
from jax.experimental import pallas as pl
from jax.experimental.pallas import tpu as pltpu
from jax.sharding import Mesh
from jax.sharding import PartitionSpec as P

X = "x"
PLANE = "plane"
CORE = "core"
TP = "tp"


def exchange(chunks, axes):
    return lax.all_to_all(chunks, axes, split_axis=0, concat_axis=0, tiled=True)


def down_kernel(line, here_ref, hidden_ref, *refs):
    weights, out_ref = refs[:-1], refs[-1]
    tp = hidden_ref.shape[0] // line
    half = tp // 2
    total = jnp.zeros(out_ref.shape, jnp.float32)
    for step in range(line):
        first = lax.rem(here_ref[0] + step, line) * tp
        for part in range(2):
            units = jnp.concatenate(
                [hidden_ref[first + part * half + i] for i in range(half)], axis=1
            )
            total += jnp.dot(
                units, weights[2 * step + part][...], preferred_element_type=jnp.float32
            )
    out_ref[...] = total.astype(out_ref.dtype)


def down_product(hidden, weights, here, line):
    column, width = hidden.shape[1], weights[0].shape[1]
    units = hidden.shape[0] * hidden.shape[2]
    vmem = pl.BlockSpec(memory_space=pltpu.VMEM)
    return pl.pallas_call(
        functools.partial(down_kernel, line),
        out_shape=jax.ShapeDtypeStruct((column, width), jnp.bfloat16),
        in_specs=[pl.BlockSpec(memory_space=pltpu.SMEM)] + [vmem] * (1 + len(weights)),
        out_specs=vmem,
        cost_estimate=pl.CostEstimate(
            flops=2 * column * units * width,
            bytes_accessed=2 * (units * width + column * width + column * units),
            transcendentals=0,
        ),
        compiler_params=pltpu.CompilerParams(vmem_limit_bytes=16 * 2**20),
    )(here.reshape(1), hidden, *weights)


def body(tokens, gate_weight, up_weight, down_weight):
    line, plane, tp = lax.axis_size(X), lax.axis_size(PLANE), lax.axis_size(TP)
    mine, width = tokens.shape
    hidden_width = 2 * gate_weight.shape[0]
    share = hidden_width // tp
    column = plane * mine
    rows = line * column
    swap = [(0, 1), (1, 0)]

    block = jnp.broadcast_to(tokens[None], (plane, mine, width))
    block = exchange(block, PLANE)
    gate_weights = (gate_weight, lax.ppermute(gate_weight, CORE, swap))
    up_weights = (up_weight, lax.ppermute(up_weight, CORE, swap))

    block, down_weight, gate_other = lax.optimization_barrier((block, down_weight, gate_weights[1]))
    gate_weights = (gate_weight, gate_other)
    block = block.reshape(column, width)
    block = exchange(jnp.broadcast_to(block[None], (line, column, width)), X)
    block = block.reshape(rows, width)
    down_weights = [down_weight] + [
        lax.ppermute(down_weight, X, [((i + step) % line, i) for i in range(line)])
        for step in range(1, line)
    ]
    down_weights = [
        part for own in down_weights for part in (own, lax.ppermute(own, CORE, swap))
    ]

    contract = (((1,), (1,)), ((), ()))
    parts = jnp.concatenate(
        [
            jnp.concatenate(
                [
                    lax.dot_general(weight, block, contract, preferred_element_type=jnp.float32)
                    for weight in pair
                ],
                axis=1,
            )
            for pair in zip(gate_weights, up_weights)
        ],
        axis=0,
    )
    parts = parts.reshape(tp, share, 2 * rows).astype(jnp.bfloat16)
    parts = exchange(parts, TP)
    sums = jnp.sum(parts.astype(jnp.float32), axis=0)
    quarter = (jax.nn.silu(sums[:, :rows]) * sums[:, rows:]).astype(jnp.bfloat16)
    quarter = quarter.T.reshape(line, 1, column, share)
    spread = jnp.broadcast_to(quarter, (line, tp, column, share))
    hidden = exchange(spread.reshape(line * tp, column, share), (X, TP))
    terms = down_product(hidden, down_weights, lax.axis_index(X), line)
    terms = exchange(terms.reshape(plane, mine, width), PLANE)
    return jnp.sum(terms.astype(jnp.float32), axis=0).astype(jnp.bfloat16)


def solution(mesh):
    line, cores = 4, 2
    fsdp, tp = mesh.devices.shape
    fine = Mesh(
        mesh.devices.reshape(line, fsdp // (line * cores), cores, tp), (X, PLANE, CORE, TP)
    )
    placed = P((X, PLANE, CORE), TP)
    return jax.shard_map(
        body, mesh=fine, in_specs=(placed,) * 4, out_specs=placed, check_vma=False
    )
```

```python
import functools

import jax
import jax.numpy as jnp
from jax import lax
from jax.experimental import pallas as pl
from jax.experimental.pallas import tpu as pltpu
from jax.sharding import Mesh
from jax.sharding import PartitionSpec as P

X = "x"
PLANE = "plane"
CORE = "core"
TP = "tp"


def exchange(chunks, axes):
    return lax.all_to_all(chunks, axes, split_axis=0, concat_axis=0, tiled=True)


def up_kernel(block_ref, *refs):
    stacks, out_ref = refs[:-1], refs[-1]
    share, each = out_ref.shape[1], out_ref.shape[0] // len(stacks)
    for at, stack_ref in enumerate(stacks):
        terms = lax.dot_general(
            stack_ref[...],
            block_ref[...],
            (((1,), (1,)), ((), ())),
            preferred_element_type=jnp.float32,
        )
        for i in range(each):
            gate = terms[i * share : (i + 1) * share]
            up = terms[(each + i) * share : (each + i + 1) * share]
            out_ref[at * each + i] = jnp.concatenate([gate, up], axis=1).astype(out_ref.dtype)


def up_product(block, stacks, tp):
    rows, width = block.shape
    units = sum(stack.shape[0] for stack in stacks)
    vmem = pl.BlockSpec(memory_space=pltpu.VMEM)
    return pl.pallas_call(
        up_kernel,
        out_shape=jax.ShapeDtypeStruct((tp, units // 2 // tp, 2 * rows), jnp.bfloat16),
        in_specs=[vmem] * (1 + len(stacks)),
        out_specs=vmem,
        cost_estimate=pl.CostEstimate(
            flops=2 * rows * units * width,
            bytes_accessed=2 * (units * width + rows * width + rows * units),
            transcendentals=0,
        ),
        compiler_params=pltpu.CompilerParams(vmem_limit_bytes=16 * 2**20),
    )(block, *stacks)


def down_kernel(line, here_ref, hidden_ref, *refs):
    weights, out_ref = refs[:-1], refs[-1]
    tp = hidden_ref.shape[0] // line
    half = tp // 2
    total = jnp.zeros(out_ref.shape, jnp.float32)
    for step in range(line):
        first = lax.rem(here_ref[0] + step, line) * tp
        for part in range(2):
            units = jnp.concatenate(
                [hidden_ref[first + part * half + i] for i in range(half)], axis=1
            )
            total += jnp.dot(
                units, weights[2 * step + part][...], preferred_element_type=jnp.float32
            )
    out_ref[...] = total.astype(out_ref.dtype)


def down_product(hidden, weights, here, line):
    column, width = hidden.shape[1], weights[0].shape[1]
    units = hidden.shape[0] * hidden.shape[2]
    vmem = pl.BlockSpec(memory_space=pltpu.VMEM)
    return pl.pallas_call(
        functools.partial(down_kernel, line),
        out_shape=jax.ShapeDtypeStruct((column, width), jnp.bfloat16),
        in_specs=[pl.BlockSpec(memory_space=pltpu.SMEM)] + [vmem] * (1 + len(weights)),
        out_specs=vmem,
        cost_estimate=pl.CostEstimate(
            flops=2 * column * units * width,
            bytes_accessed=2 * (units * width + column * width + column * units),
            transcendentals=0,
        ),
        compiler_params=pltpu.CompilerParams(vmem_limit_bytes=16 * 2**20),
    )(here.reshape(1), hidden, *weights)


def body(tokens, gate_weight, up_weight, down_weight):
    line, plane, tp = lax.axis_size(X), lax.axis_size(PLANE), lax.axis_size(TP)
    mine, width = tokens.shape
    hidden_width = 2 * gate_weight.shape[0]
    share = hidden_width // tp
    column = plane * mine
    rows = line * column
    swap = [(0, 1), (1, 0)]

    stack = jnp.concatenate([gate_weight, up_weight], axis=0)
    other_stack = lax.ppermute(stack, CORE, swap)
    block = exchange(jnp.broadcast_to(tokens[None], (plane, mine, width)), PLANE)

    block = block.reshape(column, width)
    block = exchange(jnp.broadcast_to(block[None], (line, column, width)), X)
    block = block.reshape(rows, width)
    gathered = [
        lax.ppermute(down_weight, X, [((i + step) % line, i) for i in range(line)])
        for step in range(1, line)
    ]

    block, *gathered = lax.optimization_barrier((block, *gathered))
    parts = exchange(up_product(block, (stack, other_stack), tp), TP)
    down_weights = [
        part for own in (down_weight, *gathered) for part in (own, lax.ppermute(own, CORE, swap))
    ]
    sums = jnp.sum(parts.astype(jnp.float32), axis=0)
    quarter = (jax.nn.silu(sums[:, :rows]) * sums[:, rows:]).astype(jnp.bfloat16)
    quarter = quarter.T.reshape(line, 1, column, share)
    spread = jnp.broadcast_to(quarter, (line, tp, column, share))
    hidden = exchange(spread.reshape(line * tp, column, share), (X, TP))
    terms = down_product(hidden, down_weights, lax.axis_index(X), line)
    terms = exchange(terms.reshape(plane, mine, width), PLANE)
    return jnp.sum(terms.astype(jnp.float32), axis=0).astype(jnp.bfloat16)


def solution(mesh):
    line, cores = 4, 2
    fsdp, tp = mesh.devices.shape
    fine = Mesh(
        mesh.devices.reshape(line, fsdp // (line * cores), cores, tp), (X, PLANE, CORE, TP)
    )
    placed = P((X, PLANE, CORE), TP)
    return jax.shard_map(
        body, mesh=fine, in_specs=(placed,) * 4, out_specs=placed, check_vma=False
    )
```

```python
import functools

import jax
import jax.numpy as jnp
from jax import lax
from jax.experimental import pallas as pl
from jax.experimental.pallas import tpu as pltpu
from jax.sharding import Mesh
from jax.sharding import PartitionSpec as P

X = "x"
PLANE = "plane"
CORE = "core"
TP = "tp"


def exchange(chunks, axes):
    return lax.all_to_all(chunks, axes, split_axis=0, concat_axis=0, tiled=True)


def up_kernel(block_ref, *refs):
    stacks, out_ref = refs[:-1], refs[-1]
    share, each = out_ref.shape[1], out_ref.shape[0] // len(stacks)
    for at, stack_ref in enumerate(stacks):
        terms = lax.dot_general(
            stack_ref[...],
            block_ref[...],
            (((1,), (1,)), ((), ())),
            preferred_element_type=jnp.float32,
        )
        for i in range(each):
            gate = terms[i * share : (i + 1) * share]
            up = terms[(each + i) * share : (each + i + 1) * share]
            out_ref[at * each + i] = jnp.concatenate([gate, up], axis=1).astype(out_ref.dtype)


def up_product(block, stacks, tp):
    rows, width = block.shape
    units = sum(stack.shape[0] for stack in stacks)
    vmem = pl.BlockSpec(memory_space=pltpu.VMEM)
    return pl.pallas_call(
        up_kernel,
        out_shape=jax.ShapeDtypeStruct((tp, units // 2 // tp, 2 * rows), jnp.bfloat16),
        in_specs=[vmem] * (1 + len(stacks)),
        out_specs=vmem,
        cost_estimate=pl.CostEstimate(
            flops=2 * rows * units * width,
            bytes_accessed=2 * (units * width + rows * width + rows * units),
            transcendentals=0,
        ),
        compiler_params=pltpu.CompilerParams(vmem_limit_bytes=16 * 2**20),
    )(block, *stacks)


def down_kernel(line, here_ref, hidden_ref, *refs):
    weights, out_ref = refs[:-1], refs[-1]
    tp = hidden_ref.shape[0] // line
    half = tp // 2
    total = jnp.zeros(out_ref.shape, jnp.float32)
    for step in range(line):
        first = lax.rem(here_ref[0] + step, line) * tp
        for part in range(2):
            units = jnp.concatenate(
                [hidden_ref[first + part * half + i] for i in range(half)], axis=1
            )
            total += jnp.dot(
                units, weights[2 * step + part][...], preferred_element_type=jnp.float32
            )
    out_ref[...] = total.astype(out_ref.dtype)


def down_product(hidden, weights, here, line):
    column, width = hidden.shape[1], weights[0].shape[1]
    units = hidden.shape[0] * hidden.shape[2]
    vmem = pl.BlockSpec(memory_space=pltpu.VMEM)
    return pl.pallas_call(
        functools.partial(down_kernel, line),
        out_shape=jax.ShapeDtypeStruct((column, width), jnp.bfloat16),
        in_specs=[pl.BlockSpec(memory_space=pltpu.SMEM)] + [vmem] * (1 + len(weights)),
        out_specs=vmem,
        cost_estimate=pl.CostEstimate(
            flops=2 * column * units * width,
            bytes_accessed=2 * (units * width + column * width + column * units),
            transcendentals=0,
        ),
        compiler_params=pltpu.CompilerParams(vmem_limit_bytes=16 * 2**20),
    )(here.reshape(1), hidden, *weights)


def body(tokens, gate_weight, up_weight, down_weight):
    line, plane, tp = lax.axis_size(X), lax.axis_size(PLANE), lax.axis_size(TP)
    mine, width = tokens.shape
    hidden_width = 2 * gate_weight.shape[0]
    share = hidden_width // tp
    column = plane * mine
    rows = line * column
    swap = [(0, 1), (1, 0)]

    stack = jnp.concatenate([gate_weight, up_weight], axis=0)
    other_stack = lax.ppermute(stack, CORE, swap)
    block = jnp.broadcast_to(tokens[None], (line * plane, mine, width))
    block = exchange(block, (X, PLANE)).reshape(rows, width)

    gathered = [
        lax.ppermute(down_weight, X, [((i + step) % line, i) for i in range(line)])
        for step in range(1, line)
    ]

    parts = exchange(up_product(block, (stack, other_stack), tp), TP)
    down_weights = [
        part for own in (down_weight, *gathered) for part in (own, lax.ppermute(own, CORE, swap))
    ]
    sums = jnp.sum(parts.astype(jnp.float32), axis=0)
    quarter = (jax.nn.silu(sums[:, :rows]) * sums[:, rows:]).astype(jnp.bfloat16)
    quarter = quarter.T.reshape(line, 1, column, share)
    spread = jnp.broadcast_to(quarter, (line, tp, column, share))
    hidden = exchange(spread.reshape(line * tp, column, share), (X, TP))
    terms = down_product(hidden, down_weights, lax.axis_index(X), line)
    terms = exchange(terms.reshape(plane, mine, width), PLANE)
    return jnp.sum(terms.astype(jnp.float32), axis=0).astype(jnp.bfloat16)


def solution(mesh):
    line, cores = 4, 2
    fsdp, tp = mesh.devices.shape
    fine = Mesh(
        mesh.devices.reshape(line, fsdp // (line * cores), cores, tp), (X, PLANE, CORE, TP)
    )
    placed = P((X, PLANE, CORE), TP)
    return jax.shard_map(
        body, mesh=fine, in_specs=(placed,) * 4, out_specs=placed, check_vma=False
    )
```

```python
import functools

import jax
import jax.numpy as jnp
from jax import lax
from jax.experimental import pallas as pl
from jax.experimental.pallas import tpu as pltpu
from jax.sharding import Mesh
from jax.sharding import PartitionSpec as P

X = "x"
PLANE = "plane"
CORE = "core"
TP = "tp"
STEPS = (1, 3, 2)


def exchange(chunks, axes):
    return lax.all_to_all(chunks, axes, split_axis=0, concat_axis=0, tiled=True)


def up_kernel(block_ref, *refs):
    weights, out_ref = refs[:-1], refs[-1]
    share = out_ref.shape[1]
    each = out_ref.shape[0] // 2
    block = block_ref[...].reshape(-1, block_ref.shape[-1])
    for core in range(2):
        terms = [
            lax.dot_general(
                weights[core + 2 * half][...],
                block,
                (((1,), (1,)), ((), ())),
                preferred_element_type=jnp.float32,
            )
            for half in range(2)
        ]
        for i in range(each):
            here = slice(i * share, (i + 1) * share)
            out_ref[core * each + i] = jnp.concatenate(
                [half[here] for half in terms], axis=1
            ).astype(out_ref.dtype)


def up_product(block, weights, tp):
    chips, mine, width = block.shape
    rows = chips * mine
    units = sum(weight.shape[0] for weight in weights)
    vmem = pl.BlockSpec(memory_space=pltpu.VMEM)
    return pl.pallas_call(
        up_kernel,
        out_shape=jax.ShapeDtypeStruct((tp, units // 2 // tp, 2 * rows), jnp.bfloat16),
        in_specs=[vmem] * (1 + len(weights)),
        out_specs=vmem,
        cost_estimate=pl.CostEstimate(
            flops=2 * rows * units * width,
            bytes_accessed=2 * (units * width + rows * width + rows * units),
            transcendentals=0,
        ),
        compiler_params=pltpu.CompilerParams(vmem_limit_bytes=16 * 2**20),
    )(block, *weights)


def down_kernel(line, here_ref, hidden_ref, *refs):
    weights, out_ref = refs[:-1], refs[-1]
    tp = hidden_ref.shape[0] // line
    half = tp // 2
    total = jnp.zeros(out_ref.shape, jnp.float32)
    for at, step in enumerate((0, *STEPS)):
        first = lax.rem(here_ref[0] + step, line) * tp
        for part in range(2):
            units = jnp.concatenate(
                [hidden_ref[first + part * half + i] for i in range(half)], axis=1
            )
            total += jnp.dot(
                units, weights[2 * at + part][...], preferred_element_type=jnp.float32
            )
    out_ref[...] = total.astype(out_ref.dtype)


def down_product(hidden, weights, here, line):
    column, width = hidden.shape[1], weights[0].shape[1]
    units = hidden.shape[0] * hidden.shape[2]
    vmem = pl.BlockSpec(memory_space=pltpu.VMEM)
    return pl.pallas_call(
        functools.partial(down_kernel, line),
        out_shape=jax.ShapeDtypeStruct((column, width), jnp.bfloat16),
        in_specs=[pl.BlockSpec(memory_space=pltpu.SMEM)] + [vmem] * (1 + len(weights)),
        out_specs=vmem,
        cost_estimate=pl.CostEstimate(
            flops=2 * column * units * width,
            bytes_accessed=2 * (units * width + column * width + column * units),
            transcendentals=0,
        ),
        compiler_params=pltpu.CompilerParams(vmem_limit_bytes=16 * 2**20),
    )(here.reshape(1), hidden, *weights)


def body(tokens, gate_weight, up_weight, down_weight):
    line, plane, tp = lax.axis_size(X), lax.axis_size(PLANE), lax.axis_size(TP)
    mine, width = tokens.shape
    hidden_width = 2 * gate_weight.shape[0]
    share = hidden_width // tp
    column = plane * mine
    rows = line * column
    swap = [(0, 1), (1, 0)]

    stacks = [(part, lax.ppermute(part, CORE, swap)) for part in (gate_weight, up_weight)]
    block = jnp.broadcast_to(tokens[None], (line * plane, mine, width))
    block = exchange(block, (X, PLANE))

    gathered = [
        lax.ppermute(down_weight, X, [((i + step) % line, i) for i in range(line)])
        for step in STEPS
    ]
    block, down_other = lax.optimization_barrier((block, lax.ppermute(down_weight, CORE, swap)))

    parts = exchange(up_product(block, (*stacks[0], *stacks[1]), tp), TP)
    down_weights = [down_weight, down_other] + [
        part for own in gathered for part in (own, lax.ppermute(own, CORE, swap))
    ]
    sums = jnp.sum(parts.astype(jnp.float32), axis=0)
    quarter = (jax.nn.silu(sums[:, :rows]) * sums[:, rows:]).astype(jnp.bfloat16)
    quarter = quarter.T.reshape(line, 1, column, share)
    spread = jnp.broadcast_to(quarter, (line, tp, column, share))
    hidden = exchange(spread.reshape(line * tp, column, share), (X, TP))
    terms = down_product(hidden, down_weights, lax.axis_index(X), line)
    terms = exchange(terms.reshape(plane, mine, width), PLANE)
    return jnp.sum(terms.astype(jnp.float32), axis=0).astype(jnp.bfloat16)


def solution(mesh):
    line, cores = 4, 2
    fsdp, tp = mesh.devices.shape
    fine = Mesh(
        mesh.devices.reshape(line, fsdp // (line * cores), cores, tp), (X, PLANE, CORE, TP)
    )
    placed = P((X, PLANE, CORE), TP)
    return jax.shard_map(
        body, mesh=fine, in_specs=(placed,) * 4, out_specs=placed, check_vma=False
    )
```

```python
import functools

import jax
import jax.numpy as jnp
from jax import lax
from jax.experimental import pallas as pl
from jax.experimental.pallas import tpu as pltpu
from jax.sharding import Mesh
from jax.sharding import PartitionSpec as P

X = "x"
PLANE = "plane"
CORE = "core"
TP = "tp"
STEPS = (1, 3, 2)


def exchange(chunks, axes):
    return lax.all_to_all(chunks, axes, split_axis=0, concat_axis=0, tiled=True)


def up_kernel(block_ref, *refs):
    stacks, out_ref = refs[:-1], refs[-1]
    share, each = out_ref.shape[1], out_ref.shape[0] // len(stacks)
    block = block_ref[...].reshape(-1, block_ref.shape[-1])
    for at, stack_ref in enumerate(stacks):
        terms = lax.dot_general(
            stack_ref[...],
            block,
            (((1,), (1,)), ((), ())),
            preferred_element_type=jnp.float32,
        )
        for i in range(each):
            gate = terms[i * share : (i + 1) * share]
            up = terms[(each + i) * share : (each + i + 1) * share]
            out_ref[at * each + i] = jnp.concatenate([gate, up], axis=1).astype(out_ref.dtype)


def up_product(block, stacks, tp):
    chips, mine, width = block.shape
    rows = chips * mine
    units = sum(stack.shape[0] for stack in stacks)
    vmem = pl.BlockSpec(memory_space=pltpu.VMEM)
    return pl.pallas_call(
        up_kernel,
        out_shape=jax.ShapeDtypeStruct((tp, units // 2 // tp, 2 * rows), jnp.bfloat16),
        in_specs=[vmem] * (1 + len(stacks)),
        out_specs=vmem,
        cost_estimate=pl.CostEstimate(
            flops=2 * rows * units * width,
            bytes_accessed=2 * (units * width + rows * width + rows * units),
            transcendentals=0,
        ),
        compiler_params=pltpu.CompilerParams(vmem_limit_bytes=16 * 2**20),
    )(block, *stacks)


def down_kernel(line, places, here_ref, hidden_ref, *refs):
    weights, out_ref = refs[: len(places)], refs[-1]
    tp = hidden_ref.shape[0] // line
    half = tp // 2
    total = refs[-2][...] if len(refs) > len(places) + 1 else jnp.zeros(out_ref.shape, jnp.float32)
    for (step, core), weight_ref in zip(places, weights):
        first = lax.rem(here_ref[0] + step, line) * tp + core * half
        units = jnp.concatenate([hidden_ref[first + i] for i in range(half)], axis=1)
        total += jnp.dot(units, weight_ref[...], preferred_element_type=jnp.float32)
    out_ref[...] = total.astype(out_ref.dtype)


def down_product(hidden, weights, here, line, dtype, *total):
    column, width = hidden.shape[1], next(iter(weights.values())).shape[1]
    units = sum(weight.shape[0] for weight in weights.values())
    weight_of = 1 if total else 64
    vmem = pl.BlockSpec(memory_space=pltpu.VMEM)
    return pl.pallas_call(
        functools.partial(down_kernel, line, tuple(weights)),
        out_shape=jax.ShapeDtypeStruct((column, width), dtype),
        in_specs=[pl.BlockSpec(memory_space=pltpu.SMEM)]
        + [vmem] * (1 + len(weights) + len(total)),
        out_specs=vmem,
        cost_estimate=pl.CostEstimate(
            flops=weight_of * 2 * column * units * width,
            bytes_accessed=2 * (units * width + column * width + column * units),
            transcendentals=0,
        ),
        compiler_params=pltpu.CompilerParams(vmem_limit_bytes=16 * 2**20),
    )(here.reshape(1), hidden, *weights.values(), *total)


def body(tokens, gate_weight, up_weight, down_weight):
    line, plane, tp = lax.axis_size(X), lax.axis_size(PLANE), lax.axis_size(TP)
    mine, width = tokens.shape
    hidden_width = 2 * gate_weight.shape[0]
    share = hidden_width // tp
    column = plane * mine
    rows = line * column
    swap = [(0, 1), (1, 0)]

    stack = jnp.concatenate([gate_weight, up_weight], axis=0)
    other_stack = lax.ppermute(stack, CORE, swap)
    block = jnp.broadcast_to(tokens[None], (line * plane, mine, width))
    block = exchange(block, (X, PLANE))

    gathered = [
        lax.ppermute(down_weight, X, [((i + step) % line, i) for i in range(line)])
        for step in STEPS
    ]
    block, down_other = lax.optimization_barrier((block, lax.ppermute(down_weight, CORE, swap)))
    parts = exchange(up_product(block, (stack, other_stack), tp), TP)
    sums = jnp.sum(parts.astype(jnp.float32), axis=0)
    quarter = (jax.nn.silu(sums[:, :rows]) * sums[:, rows:]).astype(jnp.bfloat16)
    quarter = quarter.T.reshape(line, 1, column, share)
    spread = jnp.broadcast_to(quarter, (line, tp, column, share))
    hidden = exchange(spread.reshape(line * tp, column, share), (X, TP))
    here = lax.axis_index(X)
    swapped = [lax.ppermute(weight, CORE, swap) for weight in gathered]
    pairs = [(down_weight, down_other), *zip(gathered, swapped)]
    places = [
        {(step, core): weight for core, weight in enumerate(pair)}
        for step, pair in zip((0, *STEPS), pairs)
    ]
    near = places[0] | places[1] | places[2]
    terms = down_product(hidden, near, here, line, jnp.float32)
    terms = down_product(hidden, places[3], here, line, jnp.bfloat16, terms)
    terms = exchange(terms.reshape(plane, mine, width), PLANE)
    return jnp.sum(terms.astype(jnp.float32), axis=0).astype(jnp.bfloat16)


def solution(mesh):
    line, cores = 4, 2
    fsdp, tp = mesh.devices.shape
    fine = Mesh(
        mesh.devices.reshape(line, fsdp // (line * cores), cores, tp), (X, PLANE, CORE, TP)
    )
    placed = P((X, PLANE, CORE), TP)
    return jax.shard_map(
        body, mesh=fine, in_specs=(placed,) * 4, out_specs=placed, check_vma=False
    )
```

```python
import functools

import jax
import jax.numpy as jnp
from jax import lax
from jax.experimental import pallas as pl
from jax.experimental.pallas import tpu as pltpu
from jax.sharding import Mesh
from jax.sharding import PartitionSpec as P

X = "x"
PLANE = "plane"
CORE = "core"
TP = "tp"
STEPS = (1, 3, 2)


def exchange(chunks, axes):
    return lax.all_to_all(chunks, axes, split_axis=0, concat_axis=0, tiled=True)


def spread_kernel(rows_ref, out_ref, held, sems):
    held[...] = jnp.broadcast_to(rows_ref[...][None], held.shape)
    size = held.shape[0]
    copies = [
        pltpu.make_async_copy(held, out_ref.at[pl.ds(i * size, size)], sems.at[i])
        for i in range(out_ref.shape[0] // size)
    ]
    for copy in copies:
        copy.start()
    for copy in copies:
        copy.wait()


def spread_rows(rows, copies, blocks):
    return pl.pallas_call(
        spread_kernel,
        out_shape=jax.ShapeDtypeStruct((copies, *rows.shape), rows.dtype),
        in_specs=[pl.BlockSpec(memory_space=pltpu.VMEM)],
        out_specs=pl.BlockSpec(memory_space=pl.ANY),
        scratch_shapes=[
            pltpu.VMEM((copies // blocks, *rows.shape), rows.dtype),
            pltpu.SemaphoreType.DMA((blocks,)),
        ],
        compiler_params=pltpu.CompilerParams(vmem_limit_bytes=8 * 2**20),
    )(rows)


def up_kernel(block_ref, *refs):
    stacks, out_ref = refs[:-1], refs[-1]
    share, each = out_ref.shape[1], out_ref.shape[0] // len(stacks)
    block = block_ref[...].reshape(-1, block_ref.shape[-1])
    for at, stack_ref in enumerate(stacks):
        terms = lax.dot_general(
            stack_ref[...],
            block,
            (((1,), (1,)), ((), ())),
            preferred_element_type=jnp.float32,
        )
        for i in range(each):
            gate = terms[i * share : (i + 1) * share]
            up = terms[(each + i) * share : (each + i + 1) * share]
            out_ref[at * each + i] = jnp.concatenate([gate, up], axis=1).astype(out_ref.dtype)


def up_product(block, stacks, tp):
    chips, mine, width = block.shape
    rows = chips * mine
    units = sum(stack.shape[0] for stack in stacks)
    vmem = pl.BlockSpec(memory_space=pltpu.VMEM)
    return pl.pallas_call(
        up_kernel,
        out_shape=jax.ShapeDtypeStruct((tp, units // 2 // tp, 2 * rows), jnp.bfloat16),
        in_specs=[vmem] * (1 + len(stacks)),
        out_specs=vmem,
        cost_estimate=pl.CostEstimate(
            flops=2 * rows * units * width,
            bytes_accessed=2 * (units * width + rows * width + rows * units),
            transcendentals=0,
        ),
        compiler_params=pltpu.CompilerParams(vmem_limit_bytes=16 * 2**20),
    )(block, *stacks)


def hidden_kernel(parts_ref, out_ref):
    line, tp, column, _ = out_ref.shape
    rows = line * column
    sums = jnp.sum(parts_ref[...].astype(jnp.float32), axis=0)
    hidden = (jax.nn.silu(sums[:, :rows]) * sums[:, rows:]).T.astype(out_ref.dtype)
    for x in range(line):
        block = hidden[x * column : (x + 1) * column]
        for i in range(tp):
            out_ref[x, i] = block


def hidden_spread(parts, line, column):
    tp, share, _ = parts.shape
    vmem = pl.BlockSpec(memory_space=pltpu.VMEM)
    return pl.pallas_call(
        hidden_kernel,
        out_shape=jax.ShapeDtypeStruct((line, tp, column, share), parts.dtype),
        in_specs=[vmem],
        out_specs=vmem,
        compiler_params=pltpu.CompilerParams(vmem_limit_bytes=8 * 2**20),
    )(parts)


def down_kernel(line, places, here_ref, hidden_ref, *refs):
    weights, out_ref = refs[: len(places)], refs[-1]
    tp = hidden_ref.shape[0] // line
    half = tp // 2
    total = refs[-2][...] if len(refs) > len(places) + 1 else jnp.zeros(out_ref.shape, jnp.float32)
    for (step, core), weight_ref in zip(places, weights):
        first = lax.rem(here_ref[0] + step, line) * tp + core * half
        units = jnp.concatenate([hidden_ref[first + i] for i in range(half)], axis=1)
        total += jnp.dot(units, weight_ref[...], preferred_element_type=jnp.float32)
    out_ref[...] = total.astype(out_ref.dtype)


def down_product(hidden, weights, here, line, dtype, *total):
    column, width = hidden.shape[1], next(iter(weights.values())).shape[1]
    units = sum(weight.shape[0] for weight in weights.values())
    weight_of = 1 if total else 64
    vmem = pl.BlockSpec(memory_space=pltpu.VMEM)
    return pl.pallas_call(
        functools.partial(down_kernel, line, tuple(weights)),
        out_shape=jax.ShapeDtypeStruct((column, width), dtype),
        in_specs=[pl.BlockSpec(memory_space=pltpu.SMEM)]
        + [vmem] * (1 + len(weights) + len(total)),
        out_specs=vmem,
        cost_estimate=pl.CostEstimate(
            flops=weight_of * 2 * column * units * width,
            bytes_accessed=2 * (units * width + column * width + column * units),
            transcendentals=0,
        ),
        compiler_params=pltpu.CompilerParams(vmem_limit_bytes=16 * 2**20),
    )(here.reshape(1), hidden, *weights.values(), *total)


def body(tokens, gate_weight, up_weight, down_weight):
    line, plane, tp = lax.axis_size(X), lax.axis_size(PLANE), lax.axis_size(TP)
    mine, width = tokens.shape
    hidden_width = 2 * gate_weight.shape[0]
    share = hidden_width // tp
    column = plane * mine
    rows = line * column
    swap = [(0, 1), (1, 0)]

    stack = jnp.concatenate([gate_weight, up_weight], axis=0)
    other_stack = lax.ppermute(stack, CORE, swap)
    block = spread_rows(tokens, line * plane, 2 * line)
    block = exchange(block, (X, PLANE))

    gathered = [
        lax.ppermute(down_weight, X, [((i + step) % line, i) for i in range(line)])
        for step in STEPS
    ]
    block, down_other = lax.optimization_barrier((block, lax.ppermute(down_weight, CORE, swap)))
    parts = exchange(up_product(block, (stack, other_stack), tp), TP)
    spread = hidden_spread(parts, line, column)
    hidden = exchange(spread.reshape(line * tp, column, share), (X, TP))
    here = lax.axis_index(X)
    swapped = [lax.ppermute(weight, CORE, swap) for weight in gathered]
    pairs = [(down_weight, down_other), *zip(gathered, swapped)]
    places = [
        {(step, core): weight for core, weight in enumerate(pair)}
        for step, pair in zip((0, *STEPS), pairs)
    ]
    near = places[0] | places[1] | places[2]
    terms = down_product(hidden, near, here, line, jnp.float32)
    terms = down_product(hidden, places[3], here, line, jnp.bfloat16, terms)
    terms = exchange(terms.reshape(plane, mine, width), PLANE)
    return jnp.sum(terms.astype(jnp.float32), axis=0).astype(jnp.bfloat16)


def solution(mesh):
    line, cores = 4, 2
    fsdp, tp = mesh.devices.shape
    fine = Mesh(
        mesh.devices.reshape(line, fsdp // (line * cores), cores, tp), (X, PLANE, CORE, TP)
    )
    placed = P((X, PLANE, CORE), TP)
    return jax.shard_map(
        body, mesh=fine, in_specs=(placed,) * 4, out_specs=placed, check_vma=False
    )
```

```python
import functools

import jax
import jax.numpy as jnp
from jax import lax
from jax.experimental import pallas as pl
from jax.experimental.pallas import tpu as pltpu
from jax.sharding import Mesh
from jax.sharding import PartitionSpec as P

X = "x"
PLANE = "plane"
CORE = "core"
TP = "tp"
STEPS = (1, 3, 2)


def exchange(chunks, axes):
    return lax.all_to_all(chunks, axes, split_axis=0, concat_axis=0, tiled=True)


def spread_kernel(rows_ref, out_ref, rows, held, row_sem, sems):
    load = pltpu.make_async_copy(rows_ref, rows, row_sem)
    load.start()
    load.wait()
    held[...] = jnp.broadcast_to(rows[...][None], held.shape)
    size = held.shape[0]
    copies = [
        pltpu.make_async_copy(held, out_ref.at[pl.ds(i * size, size)], sems.at[i])
        for i in range(out_ref.shape[0] // size)
    ]
    for copy in copies:
        copy.start()
    for copy in copies:
        copy.wait()


def spread_rows(rows, copies, blocks):
    return pl.pallas_call(
        spread_kernel,
        out_shape=jax.ShapeDtypeStruct((copies, *rows.shape), rows.dtype),
        in_specs=[pl.BlockSpec(memory_space=pltpu.HBM)],
        out_specs=pl.BlockSpec(memory_space=pl.ANY),
        scratch_shapes=[
            pltpu.VMEM(rows.shape, rows.dtype),
            pltpu.VMEM((copies // blocks, *rows.shape), rows.dtype),
            pltpu.SemaphoreType.DMA,
            pltpu.SemaphoreType.DMA((blocks,)),
        ],
        compiler_params=pltpu.CompilerParams(vmem_limit_bytes=8 * 2**20),
    )(rows)


def up_kernel(block_ref, *refs):
    stacks, out_ref = refs[:-1], refs[-1]
    share, each = out_ref.shape[1], out_ref.shape[0] // len(stacks)
    block = block_ref[...].reshape(-1, block_ref.shape[-1])
    for at, stack_ref in enumerate(stacks):
        terms = lax.dot_general(
            stack_ref[...],
            block,
            (((1,), (1,)), ((), ())),
            preferred_element_type=jnp.float32,
        )
        for i in range(each):
            gate = terms[i * share : (i + 1) * share]
            up = terms[(each + i) * share : (each + i + 1) * share]
            out_ref[at * each + i] = jnp.concatenate([gate, up], axis=1).astype(out_ref.dtype)


def up_product(block, stacks, tp):
    chips, mine, width = block.shape
    rows = chips * mine
    units = sum(stack.shape[0] for stack in stacks)
    vmem = pl.BlockSpec(memory_space=pltpu.VMEM)
    return pl.pallas_call(
        up_kernel,
        out_shape=jax.ShapeDtypeStruct((tp, units // 2 // tp, 2 * rows), jnp.bfloat16),
        in_specs=[vmem] * (1 + len(stacks)),
        out_specs=vmem,
        cost_estimate=pl.CostEstimate(
            flops=2 * rows * units * width,
            bytes_accessed=2 * (units * width + rows * width + rows * units),
            transcendentals=0,
        ),
        compiler_params=pltpu.CompilerParams(vmem_limit_bytes=16 * 2**20),
    )(block, *stacks)


def hidden_kernel(parts_ref, out_ref):
    line, tp, column, _ = out_ref.shape
    rows = line * column
    sums = jnp.sum(parts_ref[...].astype(jnp.float32), axis=0)
    hidden = (jax.nn.silu(sums[:, :rows]) * sums[:, rows:]).T.astype(out_ref.dtype)
    for x in range(line):
        block = hidden[x * column : (x + 1) * column]
        for i in range(tp):
            out_ref[x, i] = block


def hidden_spread(parts, line, column):
    tp, share, _ = parts.shape
    vmem = pl.BlockSpec(memory_space=pltpu.VMEM)
    return pl.pallas_call(
        hidden_kernel,
        out_shape=jax.ShapeDtypeStruct((line, tp, column, share), parts.dtype),
        in_specs=[vmem],
        out_specs=vmem,
        compiler_params=pltpu.CompilerParams(vmem_limit_bytes=8 * 2**20),
    )(parts)


def down_kernel(line, places, totals, moved, here_ref, hidden_ref, *refs):
    weights, more = refs[: len(places)], refs[len(places) :]
    total_refs, out_ref, room = more[:totals], more[totals], more[totals + 1 :]
    tp = hidden_ref.shape[0] // line
    half = tp // 2
    copies = [
        pltpu.make_async_copy(weights[at], room[0].at[slot], room[1].at[slot])
        for slot, at in enumerate(moved)
    ]
    for copy in copies:
        copy.start()

    def terms(at, weight):
        step, core = places[at]
        first = lax.rem(here_ref[0] + step, line) * tp + core * half
        units = jnp.concatenate([hidden_ref[first + i] for i in range(half)], axis=1)
        return jnp.dot(units, weight, preferred_element_type=jnp.float32)

    total = sum((ref[...] for ref in total_refs), jnp.zeros(out_ref.shape, jnp.float32))
    for at in range(len(places)):
        if at not in moved:
            total += terms(at, weights[at][...])
    for slot, at in enumerate(moved):
        copies[slot].wait()
        total += terms(at, room[0][slot])
    out_ref[...] = total.astype(out_ref.dtype)


def down_product(hidden, weights, here, line, dtype, *total):
    depth, width = next(iter(weights.values())).shape
    column = hidden.shape[1]
    units = depth * len(weights)
    weight_of = 1 if total else 64
    moved = [at for at, (step, core) in enumerate(weights) if step and not core and not total]
    vmem = pl.BlockSpec(memory_space=pltpu.VMEM)
    return pl.pallas_call(
        functools.partial(down_kernel, line, tuple(weights), len(total), moved),
        out_shape=jax.ShapeDtypeStruct((column, width), dtype),
        in_specs=[pl.BlockSpec(memory_space=pltpu.SMEM), vmem]
        + [pl.BlockSpec(memory_space=pl.ANY) if at in moved else vmem for at in range(len(weights))]
        + [vmem] * len(total),
        out_specs=vmem,
        scratch_shapes=[
            pltpu.VMEM((len(moved), depth, width), hidden.dtype),
            pltpu.SemaphoreType.DMA((len(moved),)),
        ]
        if moved
        else [],
        cost_estimate=pl.CostEstimate(
            flops=weight_of * 2 * column * units * width,
            bytes_accessed=2 * (units * width + column * width + column * units),
            transcendentals=0,
        ),
        compiler_params=pltpu.CompilerParams(vmem_limit_bytes=16 * 2**20),
    )(here.reshape(1), hidden, *weights.values(), *total)


def body(tokens, gate_weight, up_weight, down_weight):
    line, plane, tp = lax.axis_size(X), lax.axis_size(PLANE), lax.axis_size(TP)
    mine, width = tokens.shape
    hidden_width = 2 * gate_weight.shape[0]
    share = hidden_width // tp
    column = plane * mine
    rows = line * column
    swap = [(0, 1), (1, 0)]

    stack = jnp.concatenate([gate_weight, up_weight], axis=0)
    other_stack = lax.ppermute(stack, CORE, swap)
    block = spread_rows(pltpu.with_memory_space_constraint(tokens, pltpu.HBM), line * plane, 2 * line)
    block = exchange(block, (X, PLANE))

    gathered = [
        lax.ppermute(down_weight, X, [((i + step) % line, i) for i in range(line)])
        for step in STEPS
    ]
    block, down_other = lax.optimization_barrier((block, lax.ppermute(down_weight, CORE, swap)))
    parts = exchange(up_product(block, (stack, other_stack), tp), TP)
    spread = hidden_spread(parts, line, column)
    hidden = exchange(spread.reshape(line * tp, column, share), (X, TP))
    here = lax.axis_index(X)
    swapped = [lax.ppermute(weight, CORE, swap) for weight in gathered]
    pairs = [(down_weight, down_other), *zip(gathered, swapped)]
    places = [
        {(step, core): weight for core, weight in enumerate(pair)}
        for step, pair in zip((0, *STEPS), pairs)
    ]
    near = places[0] | places[1] | places[2]
    terms = down_product(hidden, near, here, line, jnp.float32)
    terms = down_product(hidden, places[3], here, line, jnp.bfloat16, terms)
    terms = exchange(terms.reshape(plane, mine, width), PLANE)
    return jnp.sum(terms.astype(jnp.float32), axis=0).astype(jnp.bfloat16)


def solution(mesh):
    line, cores = 4, 2
    fsdp, tp = mesh.devices.shape
    fine = Mesh(
        mesh.devices.reshape(line, fsdp // (line * cores), cores, tp), (X, PLANE, CORE, TP)
    )
    placed = P((X, PLANE, CORE), TP)
    return jax.shard_map(
        body, mesh=fine, in_specs=(placed,) * 4, out_specs=placed, check_vma=False
    )
```

```python
import functools

import jax
import jax.numpy as jnp
from jax import lax
from jax.experimental import pallas as pl
from jax.experimental.pallas import tpu as pltpu
from jax.sharding import Mesh
from jax.sharding import PartitionSpec as P

X = "x"
PLANE = "plane"
CORE = "core"
TP = "tp"
STEPS = (1, 3, 2)


def exchange(chunks, axes):
    return lax.all_to_all(chunks, axes, split_axis=0, concat_axis=0, tiled=True)


def spread_kernel(rows_ref, out_ref, held, sems):
    held[...] = jnp.broadcast_to(rows_ref[...][None], held.shape)
    size = held.shape[0]
    copies = [
        pltpu.make_async_copy(held, out_ref.at[pl.ds(i * size, size)], sems.at[i])
        for i in range(out_ref.shape[0] // size)
    ]
    for copy in copies:
        copy.start()
    for copy in copies:
        copy.wait()


def spread_rows(rows, copies, blocks):
    return pl.pallas_call(
        spread_kernel,
        out_shape=jax.ShapeDtypeStruct((copies, *rows.shape), rows.dtype),
        in_specs=[pl.BlockSpec(memory_space=pltpu.VMEM)],
        out_specs=pl.BlockSpec(memory_space=pl.ANY),
        scratch_shapes=[
            pltpu.VMEM((copies // blocks, *rows.shape), rows.dtype),
            pltpu.SemaphoreType.DMA((blocks,)),
        ],
        compiler_params=pltpu.CompilerParams(vmem_limit_bytes=8 * 2**20),
    )(rows)


def up_kernel(block_ref, *refs):
    stacks, out_ref = refs[:-1], refs[-1]
    share, each = out_ref.shape[1], out_ref.shape[0] // len(stacks)
    block = block_ref[...].reshape(-1, block_ref.shape[-1])
    for at, stack_ref in enumerate(stacks):
        terms = lax.dot_general(
            stack_ref[...],
            block,
            (((1,), (1,)), ((), ())),
            preferred_element_type=jnp.float32,
        )
        for i in range(each):
            gate = terms[i * share : (i + 1) * share]
            up = terms[(each + i) * share : (each + i + 1) * share]
            out_ref[at * each + i] = jnp.concatenate([gate, up], axis=1).astype(out_ref.dtype)


def up_product(block, stacks, tp):
    chips, mine, width = block.shape
    rows = chips * mine
    units = sum(stack.shape[0] for stack in stacks)
    vmem = pl.BlockSpec(memory_space=pltpu.VMEM)
    return pl.pallas_call(
        up_kernel,
        out_shape=jax.ShapeDtypeStruct((tp, units // 2 // tp, 2 * rows), jnp.bfloat16),
        in_specs=[vmem] * (1 + len(stacks)),
        out_specs=vmem,
        cost_estimate=pl.CostEstimate(
            flops=2 * rows * units * width,
            bytes_accessed=2 * (units * width + rows * width + rows * units),
            transcendentals=0,
        ),
        compiler_params=pltpu.CompilerParams(vmem_limit_bytes=16 * 2**20),
    )(block, *stacks)


def hidden_kernel(parts_ref, out_ref):
    tp, line, column, _ = out_ref.shape
    rows = line * column
    sums = jnp.sum(parts_ref[...].astype(jnp.float32), axis=0)
    hidden = (jax.nn.silu(sums[:, :rows]) * sums[:, rows:]).T.astype(out_ref.dtype)
    for x in range(line):
        block = hidden[x * column : (x + 1) * column]
        for i in range(tp):
            out_ref[i, x] = block


def hidden_spread(parts, line, column):
    tp, share, _ = parts.shape
    vmem = pl.BlockSpec(memory_space=pltpu.VMEM)
    return pl.pallas_call(
        hidden_kernel,
        out_shape=jax.ShapeDtypeStruct((tp, line, column, share), parts.dtype),
        in_specs=[vmem],
        out_specs=vmem,
        compiler_params=pltpu.CompilerParams(vmem_limit_bytes=8 * 2**20),
    )(parts)


def down_kernel(line, places, here_ref, hidden_ref, *refs):
    weights, out_ref = refs[: len(places)], refs[-1]
    tp = hidden_ref.shape[0] // line
    half = tp // 2
    total = refs[-2][...] if len(refs) > len(places) + 1 else jnp.zeros(out_ref.shape, jnp.float32)
    for (step, core), weight_ref in zip(places, weights):
        first = lax.rem(here_ref[0] + step, line) + core * half * line
        units = jnp.concatenate([hidden_ref[first + i * line] for i in range(half)], axis=1)
        total += jnp.dot(units, weight_ref[...], preferred_element_type=jnp.float32)
    out_ref[...] = total.astype(out_ref.dtype)


def down_product(hidden, weights, here, line, dtype, *total):
    column, width = hidden.shape[1], next(iter(weights.values())).shape[1]
    units = sum(weight.shape[0] for weight in weights.values())
    weight_of = 1 if total else 64
    vmem = pl.BlockSpec(memory_space=pltpu.VMEM)
    return pl.pallas_call(
        functools.partial(down_kernel, line, tuple(weights)),
        out_shape=jax.ShapeDtypeStruct((column, width), dtype),
        in_specs=[pl.BlockSpec(memory_space=pltpu.SMEM)]
        + [vmem] * (1 + len(weights) + len(total)),
        out_specs=vmem,
        cost_estimate=pl.CostEstimate(
            flops=weight_of * 2 * column * units * width,
            bytes_accessed=2 * (units * width + column * width + column * units),
            transcendentals=0,
        ),
        compiler_params=pltpu.CompilerParams(vmem_limit_bytes=16 * 2**20),
    )(here.reshape(1), hidden, *weights.values(), *total)


def body(tokens, gate_weight, up_weight, down_weight):
    line, plane, tp = lax.axis_size(X), lax.axis_size(PLANE), lax.axis_size(TP)
    mine, width = tokens.shape
    hidden_width = 2 * gate_weight.shape[0]
    share = hidden_width // tp
    column = plane * mine
    rows = line * column
    swap = [(0, 1), (1, 0)]

    stack = jnp.concatenate([gate_weight, up_weight], axis=0)
    other_stack = lax.ppermute(stack, CORE, swap)
    block = spread_rows(tokens, line * plane, 2 * line)
    block = exchange(block, (X, PLANE))

    gathered = [
        lax.ppermute(down_weight, X, [((i + step) % line, i) for i in range(line)])
        for step in STEPS
    ]
    block, down_other = lax.optimization_barrier((block, lax.ppermute(down_weight, CORE, swap)))
    parts = exchange(up_product(block, (stack, other_stack), tp), TP)
    spread = hidden_spread(parts, line, column)
    hidden = exchange(spread.reshape(tp * line, column, share), (TP, X))
    here = lax.axis_index(X)
    swapped = [lax.ppermute(weight, CORE, swap) for weight in gathered]
    pairs = [(down_weight, down_other), *zip(gathered, swapped)]
    places = [
        {(step, core): weight for core, weight in enumerate(pair)}
        for step, pair in zip((0, *STEPS), pairs)
    ]
    near = places[0] | places[1] | places[2]
    terms = down_product(hidden, near, here, line, jnp.float32)
    terms = down_product(hidden, places[3], here, line, jnp.bfloat16, terms)
    terms = exchange(terms.reshape(plane, mine, width), PLANE)
    return jnp.sum(terms.astype(jnp.float32), axis=0).astype(jnp.bfloat16)


def solution(mesh):
    line, cores = 4, 2
    fsdp, tp = mesh.devices.shape
    fine = Mesh(
        mesh.devices.reshape(line, fsdp // (line * cores), cores, tp), (X, PLANE, CORE, TP)
    )
    placed = P((X, PLANE, CORE), TP)
    return jax.shard_map(
        body, mesh=fine, in_specs=(placed,) * 4, out_specs=placed, check_vma=False
    )
```

```python
import functools

import jax
import jax.numpy as jnp
from jax import lax
from jax.experimental import pallas as pl
from jax.experimental.pallas import tpu as pltpu
from jax.sharding import Mesh
from jax.sharding import PartitionSpec as P

X = "x"
PLANE = "plane"
CORE = "core"
TP = "tp"
STEPS = (1, 3, 2)


def exchange(chunks, axes):
    return lax.all_to_all(chunks, axes, split_axis=0, concat_axis=0, tiled=True)


def spread_kernel(rows_ref, out_ref, held, sems):
    held[...] = jnp.broadcast_to(rows_ref[...][None], held.shape)
    size = held.shape[0]
    copies = [
        pltpu.make_async_copy(held, out_ref.at[pl.ds(i * size, size)], sems.at[i])
        for i in range(out_ref.shape[0] // size)
    ]
    for copy in copies:
        copy.start()
    for copy in copies:
        copy.wait()


def spread_rows(rows, copies, blocks):
    return pl.pallas_call(
        spread_kernel,
        out_shape=jax.ShapeDtypeStruct((copies, *rows.shape), rows.dtype),
        in_specs=[pl.BlockSpec(memory_space=pltpu.VMEM)],
        out_specs=pl.BlockSpec(memory_space=pl.ANY),
        scratch_shapes=[
            pltpu.VMEM((copies // blocks, *rows.shape), rows.dtype),
            pltpu.SemaphoreType.DMA((blocks,)),
        ],
        compiler_params=pltpu.CompilerParams(vmem_limit_bytes=8 * 2**20),
    )(rows)


def up_kernel(line, block_ref, *refs):
    stacks, out_ref = refs[:-1], refs[-1]
    share, each = out_ref.shape[1], out_ref.shape[0] // len(stacks)
    chips, mine, width = block_ref.shape
    block = block_ref[...].reshape(chips // line, line, mine, width)
    block = jnp.concatenate(
        [block[:, x].reshape(chips // line * mine, width) for x in range(line)], axis=0
    )
    for at, stack_ref in enumerate(stacks):
        terms = lax.dot_general(
            stack_ref[...],
            block,
            (((1,), (1,)), ((), ())),
            preferred_element_type=jnp.float32,
        )
        for i in range(each):
            gate = terms[i * share : (i + 1) * share]
            up = terms[(each + i) * share : (each + i + 1) * share]
            out_ref[at * each + i] = jnp.concatenate([gate, up], axis=1).astype(out_ref.dtype)


def up_product(block, stacks, tp, line):
    chips, mine, width = block.shape
    rows = chips * mine
    units = sum(stack.shape[0] for stack in stacks)
    vmem = pl.BlockSpec(memory_space=pltpu.VMEM)
    return pl.pallas_call(
        functools.partial(up_kernel, line),
        out_shape=jax.ShapeDtypeStruct((tp, units // 2 // tp, 2 * rows), jnp.bfloat16),
        in_specs=[vmem] * (1 + len(stacks)),
        out_specs=vmem,
        cost_estimate=pl.CostEstimate(
            flops=2 * rows * units * width,
            bytes_accessed=2 * (units * width + rows * width + rows * units),
            transcendentals=0,
        ),
        compiler_params=pltpu.CompilerParams(vmem_limit_bytes=16 * 2**20),
    )(block, *stacks)


def hidden_kernel(parts_ref, out_ref):
    tp, line, column, _ = out_ref.shape
    rows = line * column
    sums = jnp.sum(parts_ref[...].astype(jnp.float32), axis=0)
    hidden = (jax.nn.silu(sums[:, :rows]) * sums[:, rows:]).T.astype(out_ref.dtype)
    for x in range(line):
        block = hidden[x * column : (x + 1) * column]
        for i in range(tp):
            out_ref[i, x] = block


def hidden_spread(parts, line, column):
    tp, share, _ = parts.shape
    vmem = pl.BlockSpec(memory_space=pltpu.VMEM)
    return pl.pallas_call(
        hidden_kernel,
        out_shape=jax.ShapeDtypeStruct((tp, line, column, share), parts.dtype),
        in_specs=[vmem],
        out_specs=vmem,
        compiler_params=pltpu.CompilerParams(vmem_limit_bytes=8 * 2**20),
    )(parts)


def down_kernel(line, places, here_ref, hidden_ref, *refs):
    weights, out_ref = refs[: len(places)], refs[-1]
    tp = hidden_ref.shape[0] // line
    half = tp // 2
    total = refs[-2][...] if len(refs) > len(places) + 1 else jnp.zeros(out_ref.shape, jnp.float32)
    for (step, core), weight_ref in zip(places, weights):
        first = lax.rem(here_ref[0] + step, line) + core * half * line
        units = jnp.concatenate([hidden_ref[first + i * line] for i in range(half)], axis=1)
        total += jnp.dot(units, weight_ref[...], preferred_element_type=jnp.float32)
    out_ref[...] = total.astype(out_ref.dtype)


def down_product(hidden, weights, here, line, dtype, *total):
    column, width = hidden.shape[1], next(iter(weights.values())).shape[1]
    units = sum(weight.shape[0] for weight in weights.values())
    weight_of = 1 if total else 64
    vmem = pl.BlockSpec(memory_space=pltpu.VMEM)
    return pl.pallas_call(
        functools.partial(down_kernel, line, tuple(weights)),
        out_shape=jax.ShapeDtypeStruct((column, width), dtype),
        in_specs=[pl.BlockSpec(memory_space=pltpu.SMEM)]
        + [vmem] * (1 + len(weights) + len(total)),
        out_specs=vmem,
        cost_estimate=pl.CostEstimate(
            flops=weight_of * 2 * column * units * width,
            bytes_accessed=2 * (units * width + column * width + column * units),
            transcendentals=0,
        ),
        compiler_params=pltpu.CompilerParams(vmem_limit_bytes=16 * 2**20),
    )(here.reshape(1), hidden, *weights.values(), *total)


def body(tokens, gate_weight, up_weight, down_weight):
    line, plane, tp = lax.axis_size(X), lax.axis_size(PLANE), lax.axis_size(TP)
    mine, width = tokens.shape
    hidden_width = 2 * gate_weight.shape[0]
    share = hidden_width // tp
    column = plane * mine
    rows = line * column
    swap = [(0, 1), (1, 0)]

    stack = jnp.concatenate([gate_weight, up_weight], axis=0)
    other_stack = lax.ppermute(stack, CORE, swap)
    block = spread_rows(tokens, line * plane, 2 * line)
    block = exchange(block, (PLANE, X))

    gathered = [
        lax.ppermute(down_weight, X, [((i + step) % line, i) for i in range(line)])
        for step in STEPS
    ]
    block, down_other = lax.optimization_barrier((block, lax.ppermute(down_weight, CORE, swap)))
    parts = exchange(up_product(block, (stack, other_stack), tp, line), TP)
    spread = hidden_spread(parts, line, column)
    hidden = exchange(spread.reshape(tp * line, column, share), (TP, X))
    here = lax.axis_index(X)
    swapped = [lax.ppermute(weight, CORE, swap) for weight in gathered]
    pairs = [(down_weight, down_other), *zip(gathered, swapped)]
    places = [
        {(step, core): weight for core, weight in enumerate(pair)}
        for step, pair in zip((0, *STEPS), pairs)
    ]
    near = places[0] | places[1] | places[2]
    terms = down_product(hidden, near, here, line, jnp.float32)
    terms = down_product(hidden, places[3], here, line, jnp.bfloat16, terms)
    terms = exchange(terms.reshape(plane, mine, width), PLANE)
    return jnp.sum(terms.astype(jnp.float32), axis=0).astype(jnp.bfloat16)


def solution(mesh):
    line, cores = 4, 2
    fsdp, tp = mesh.devices.shape
    fine = Mesh(
        mesh.devices.reshape(line, fsdp // (line * cores), cores, tp), (X, PLANE, CORE, TP)
    )
    placed = P((X, PLANE, CORE), TP)
    return jax.shard_map(
        body, mesh=fine, in_specs=(placed,) * 4, out_specs=placed, check_vma=False
    )
```

```python
import functools

import jax
import jax.numpy as jnp
from jax import lax
from jax.experimental import pallas as pl
from jax.experimental.pallas import tpu as pltpu
from jax.sharding import Mesh
from jax.sharding import PartitionSpec as P

X = "x"
PLANE = "plane"
CORE = "core"
TP = "tp"
STEPS = (1, 3, 2)


def exchange(chunks, axes):
    return lax.all_to_all(chunks, axes, split_axis=0, concat_axis=0, tiled=True)


def spread_kernel(rows_ref, out_ref, held, sems):
    held[...] = jnp.broadcast_to(rows_ref[...][None], held.shape)
    size = held.shape[0]
    copies = [
        pltpu.make_async_copy(held, out_ref.at[pl.ds(i * size, size)], sems.at[i])
        for i in range(out_ref.shape[0] // size)
    ]
    for copy in copies:
        copy.start()
    for copy in copies:
        copy.wait()


def spread_rows(rows, copies, blocks):
    return pl.pallas_call(
        spread_kernel,
        out_shape=jax.ShapeDtypeStruct((copies, *rows.shape), rows.dtype),
        in_specs=[pl.BlockSpec(memory_space=pltpu.VMEM)],
        out_specs=pl.BlockSpec(memory_space=pl.ANY),
        scratch_shapes=[
            pltpu.VMEM((copies // blocks, *rows.shape), rows.dtype),
            pltpu.SemaphoreType.DMA((blocks,)),
        ],
        compiler_params=pltpu.CompilerParams(vmem_limit_bytes=8 * 2**20),
    )(rows)


def up_kernel(block_ref, *refs):
    stacks, out_ref = refs[:-1], refs[-1]
    share, each = out_ref.shape[1], out_ref.shape[0] // len(stacks)
    block = block_ref[...].reshape(-1, block_ref.shape[-1])
    for at, stack_ref in enumerate(stacks):
        terms = lax.dot_general(
            stack_ref[...],
            block,
            (((1,), (1,)), ((), ())),
            preferred_element_type=jnp.float32,
        )
        for i in range(each):
            gate = terms[i * share : (i + 1) * share]
            up = terms[(each + i) * share : (each + i + 1) * share]
            out_ref[at * each + i] = jnp.concatenate([gate, up], axis=1).astype(out_ref.dtype)


def up_product(block, stacks, tp):
    chips, mine, width = block.shape
    rows = chips * mine
    units = sum(stack.shape[0] for stack in stacks)
    vmem = pl.BlockSpec(memory_space=pltpu.VMEM)
    return pl.pallas_call(
        up_kernel,
        out_shape=jax.ShapeDtypeStruct((tp, units // 2 // tp, 2 * rows), jnp.bfloat16),
        in_specs=[vmem] * (1 + len(stacks)),
        out_specs=vmem,
        cost_estimate=pl.CostEstimate(
            flops=2 * rows * units * width,
            bytes_accessed=2 * (units * width + rows * width + rows * units),
            transcendentals=0,
        ),
        compiler_params=pltpu.CompilerParams(vmem_limit_bytes=16 * 2**20),
    )(block, *stacks)


def hidden_kernel(parts_ref, out_ref):
    tp, line, column, _ = out_ref.shape
    rows = line * column
    sums = jnp.sum(parts_ref[...].astype(jnp.float32), axis=0)
    hidden = (jax.nn.silu(sums[:, :rows]) * sums[:, rows:]).T.astype(out_ref.dtype)
    for x in range(line):
        block = hidden[x * column : (x + 1) * column]
        for i in range(tp):
            out_ref[i, x] = block


def hidden_spread(parts, line, column):
    tp, share, _ = parts.shape
    vmem = pl.BlockSpec(memory_space=pltpu.VMEM)
    return pl.pallas_call(
        hidden_kernel,
        out_shape=jax.ShapeDtypeStruct((tp, line, column, share), parts.dtype),
        in_specs=[vmem],
        out_specs=vmem,
        compiler_params=pltpu.CompilerParams(vmem_limit_bytes=8 * 2**20),
    )(parts)


def down_kernel(line, places, here_ref, hidden_ref, *refs):
    weights, out_ref = refs[: len(places)], refs[-1]
    tp = hidden_ref.shape[0] // line
    half = tp // 2
    total = refs[-2][...] if len(refs) > len(places) + 1 else jnp.zeros(out_ref.shape, jnp.float32)
    for (step, core), weight_ref in zip(places, weights):
        first = lax.rem(here_ref[0] + step, line) + core * half * line
        units = jnp.concatenate([hidden_ref[first + i * line] for i in range(half)], axis=1)
        total += jnp.dot(units, weight_ref[...], preferred_element_type=jnp.float32)
    out_ref[...] = total.astype(out_ref.dtype)


def down_product(hidden, weights, here, line, dtype, *total):
    column, width = hidden.shape[1], next(iter(weights.values())).shape[1]
    units = sum(weight.shape[0] for weight in weights.values())
    weight_of = 1 if total else 64
    vmem = pl.BlockSpec(memory_space=pltpu.VMEM)
    return pl.pallas_call(
        functools.partial(down_kernel, line, tuple(weights)),
        out_shape=jax.ShapeDtypeStruct((column, width), dtype),
        in_specs=[pl.BlockSpec(memory_space=pltpu.SMEM)]
        + [vmem] * (1 + len(weights) + len(total)),
        out_specs=vmem,
        cost_estimate=pl.CostEstimate(
            flops=weight_of * 2 * column * units * width,
            bytes_accessed=2 * (units * width + column * width + column * units),
            transcendentals=0,
        ),
        compiler_params=pltpu.CompilerParams(vmem_limit_bytes=16 * 2**20),
    )(here.reshape(1), hidden, *weights.values(), *total)


def body(tokens, gate_weight, up_weight, down_weight):
    line, plane, tp = lax.axis_size(X), lax.axis_size(PLANE), lax.axis_size(TP)
    mine, width = tokens.shape
    hidden_width = 2 * gate_weight.shape[0]
    share = hidden_width // tp
    column = plane * mine
    rows = line * column
    swap = [(0, 1), (1, 0)]

    stack = jnp.concatenate([gate_weight, up_weight], axis=0)
    other_stack = lax.ppermute(stack, CORE, swap)
    block = spread_rows(tokens, line * plane, 2 * line)
    block = exchange(block, (X, PLANE))

    gathered = [
        lax.ppermute(down_weight, X, [((i + step) % line, i) for i in range(line)])
        for step in STEPS
    ]
    block, down_other = lax.optimization_barrier((block, lax.ppermute(down_weight, CORE, swap)))
    parts = exchange(up_product(block, (stack, other_stack), tp), TP)
    spread = hidden_spread(parts, line, column)
    hidden = exchange(spread.reshape(tp * line, column, share), (TP, X))
    here = lax.axis_index(X)
    swapped = [lax.ppermute(weight, CORE, swap) for weight in gathered]
    pairs = [(down_weight, down_other), *zip(gathered, swapped)]
    places = [
        {(step, core): weight for core, weight in enumerate(pair)}
        for step, pair in zip((0, *STEPS), pairs)
    ]
    near = places[0] | places[1] | {(STEPS[1], 0): gathered[1]}
    far = {(STEPS[1], 1): swapped[1]} | places[3]
    terms = down_product(hidden, near, here, line, jnp.float32)
    terms = down_product(hidden, far, here, line, jnp.bfloat16, terms)
    terms = exchange(terms.reshape(plane, mine, width), PLANE)
    return jnp.sum(terms.astype(jnp.float32), axis=0).astype(jnp.bfloat16)


def solution(mesh):
    line, cores = 4, 2
    fsdp, tp = mesh.devices.shape
    fine = Mesh(
        mesh.devices.reshape(line, fsdp // (line * cores), cores, tp), (X, PLANE, CORE, TP)
    )
    placed = P((X, PLANE, CORE), TP)
    return jax.shard_map(
        body, mesh=fine, in_specs=(placed,) * 4, out_specs=placed, check_vma=False
    )
```
